512 devices in a mesh: seq: 128 (over z, y, core), head: 4 (over x).
Axes of the slice: x: 4, y: 8, z: 8, core: 2. Of those that a mesh axis runs over, the one named last changes fastest.
Arguments:
- queries: bfloat16 [16384, 2048], P('seq', 'head'), may hold values from -1.25 to 1.25
- key_vectors: bfloat16 [16384, 2048], P('seq', 'head'), may hold values from -1.25 to 1.25
- value_vectors: bfloat16 [16384, 2048], P('seq', 'head'), may hold values from -4 to 4
- feature_proj: bfloat16 [16, 128, 256], P('head'), may hold values from -2.5 to 2.5
- out_weight: bfloat16 [2048, 2048], P('head'), may hold values from -0.1875 to 0.1875
- grad_output: bfloat16 [16384, 2048], P('seq', 'head'), may hold values from -4 to 4
Outputs:
- layer_out: bfloat16 [16384, 2048], P('seq', 'head')
- grad_queries: bfloat16 [16384, 2048], P('seq', 'head')
- grad_keys: bfloat16 [16384, 2048], P('seq', 'head')
- grad_values: bfloat16 [16384, 2048], P('seq', 'head')
The draws below stay inside these ranges and needn't reach their ends.
All inputs are finite; a program needn't handle non-finite values.
Results may differ from the reference program's by a relative error of at most 0.025.
Values may be sent and summed in bfloat16 or wider, within the bound.
A program may use at most 128 MiB of HBM per device.

```python
import jax
import jax.numpy as jnp
from jax import lax

HEADS = 16
HEAD_DIM = 128
FEATURES = 256
DW = 2048
BLOCK = 128
HD = 2048
TOKENS = 16384


def raised(drawn, stream_key, source, target, blocks, factor):
    owner, partner = [(jnp.arange(drawn.shape[axis_at]) // (drawn.shape[axis_at] // blocks)).reshape([-1 if axis == axis_at else 1 for axis in range(drawn.ndim)]) for axis_at in (source, target)]
    chosen = jax.random.permutation(stream_key, blocks)[partner]
    strong = (owner == chosen) | (owner == (partner + blocks // 2) % blocks)
    return jnp.where(strong, factor * drawn, drawn)


def steps_of(key, dims, split, smallest, top_value):
    gain = 1.0
    for position, parts in split:
        heights = jax.random.uniform(jax.random.fold_in(jax.random.fold_in(key, 6), position), (parts,), jnp.float32, smallest / len(split), top_value / len(split))
        gain = gain * jnp.repeat(jnp.exp(heights), dims[position] // parts).reshape((-1,) + (1,) * (len(dims) - 1 - position))
    return gain


def gaussian(own_key, shape, deviation, limit, shards=(), kind=jnp.bfloat16):
    drawn = deviation * jax.random.normal(own_key, shape, jnp.float32)
    if shards:
        drawn = drawn * steps_of(own_key, shape, shards, -0.22, 0.18)
    return jnp.clip(drawn, -limit, limit).astype(kind)


def bell_draw_with(own_key, shape, spread, limit, pieces, heavy, held_as=jnp.bfloat16):
    array = spread * jax.random.normal(own_key, shape, jnp.float32)
    if pieces:
        array = array * steps_of(own_key, shape, pieces, -0.22, 0.18)
    return jnp.clip(raised(array, jax.random.fold_in(own_key, 3), *heavy), -limit, limit).astype(held_as)


def setup_inputs(seed: int = 0) -> dict:
    streams_of = jax.random.split(jax.random.key(seed), 7)
    queries = gaussian(streams_of[0], (TOKENS, HD), 0.5, 1.25, ((0, 128), (1, 4)))
    key_vectors = gaussian(streams_of[1], (TOKENS, HD), 0.5, 1.25, ((0, 128), (1, 4)))
    value_vectors = gaussian(streams_of[2], (TOKENS, HD), 1.0, 4.0, ((0, 128), (1, 4)))
    feature_proj = gaussian(streams_of[3], (HEADS, HEAD_DIM, FEATURES), 1.0, 2.5, ((0, 4),))
    out_weight = bell_draw_with(streams_of[4], (HD, DW), HD ** -0.5, 0.1875, ((0, 4),), (0, 1, 4, 2.0))
    grad_output = gaussian(streams_of[5], (TOKENS, DW), 1.0, 4.0, ((0, 128), (1, 4)))
    return dict(queries=queries, key_vectors=key_vectors, value_vectors=value_vectors, feature_proj=feature_proj, out_weight=out_weight, grad_output=grad_output)


epsilon = 1e-05

def lower_mask(width):
    row_ids = lax.broadcasted_iota(jnp.int32, (width, width), 0)
    col_ids = lax.broadcasted_iota(jnp.int32, (width, width), 1)
    return col_ids <= row_ids

def rounded(values):
    return lax.optimization_barrier(values.astype(jnp.bfloat16)).astype(jnp.float32)

def reference(queries, key_vectors, value_vectors, feature_proj, out_weight, grad_output):
    feat_scale = HEAD_DIM ** (-0.25)
    n_blocks = TOKENS // BLOCK
    causal = lower_mask(BLOCK)

    def one_head(packed):
        q_head, k_head, v_head, omega, w_rows = packed
        q_feat32 = jnp.exp(jnp.dot(q_head, omega, preferred_element_type=jnp.float32) * feat_scale)
        k_wide = k_head.astype(jnp.float32)
        half_sq = lax.optimization_barrier(jnp.sum(k_wide * k_wide, axis=1, keepdims=True)) * (feat_scale * feat_scale * 0.5)
        k_feat32 = jnp.exp(jnp.dot(k_head, omega, preferred_element_type=jnp.float32) * feat_scale - half_sq)
        q_blocks = rounded(q_feat32).reshape(n_blocks, BLOCK, FEATURES)
        k_blocks = rounded(k_feat32).reshape(n_blocks, BLOCK, FEATURES)
        v_blocks = v_head.astype(jnp.float32).reshape(n_blocks, BLOCK, HEAD_DIM)
        states = jnp.einsum('ncm,ncd->nmd', k_blocks, v_blocks)
        running = jnp.cumsum(states, axis=0)
        zero_state = jnp.zeros((1, FEATURES, HEAD_DIM), jnp.float32)
        carried = jnp.concatenate([zero_state, running[:-1]], axis=0)
        carried_b = rounded(carried)
        scores = jnp.where(causal, jnp.einsum('nim,njm->nij', q_blocks, k_blocks), 0.0)
        scores_b = rounded(scores)
        numerator = jnp.einsum('nij,njd->nid', scores_b, v_blocks) + jnp.einsum('nim,nmd->nid', q_blocks, carried_b)
        row_root = jnp.sqrt(lax.optimization_barrier(jnp.mean(numerator * numerator, axis=2, keepdims=True)) + epsilon)
        normed = numerator / row_root
        mixed_head = normed.astype(jnp.bfloat16).reshape(TOKENS, HEAD_DIM)
        grad_mixed = lax.dot_general(grad_output, w_rows, (((1,), (1,)), ((), ())), preferred_element_type=jnp.float32)
        grad_mixed = grad_mixed.reshape(n_blocks, BLOCK, HEAD_DIM)
        grad_numer = (grad_mixed - normed * lax.optimization_barrier(jnp.mean(grad_mixed * normed, axis=2, keepdims=True))) / row_root
        grad_numer_b = rounded(grad_numer)
        later_terms = jnp.einsum('nim,nid->nmd', q_blocks, grad_numer_b)
        backward_sum = jnp.cumsum(later_terms[::-1], axis=0)[::-1]
        after_sum = jnp.concatenate([backward_sum[1:], zero_state], axis=0)
        after_b = rounded(after_sum)
        grad_scores = rounded(jnp.where(causal, jnp.einsum('nid,njd->nij', grad_numer_b, v_blocks), 0.0))
        grad_v = jnp.einsum('nij,nid->njd', scores_b, grad_numer_b) + jnp.einsum('njm,nmd->njd', k_blocks, after_b)
        grad_qf = jnp.einsum('nij,njm->nim', grad_scores, k_blocks) + jnp.einsum('nid,nmd->nim', grad_numer_b, carried_b)
        grad_kf = jnp.einsum('nij,nim->njm', grad_scores, q_blocks) + jnp.einsum('njd,nmd->njm', v_blocks, after_b)
        query_terms = (grad_qf.reshape(TOKENS, FEATURES) * q_feat32).astype(jnp.bfloat16)
        key_terms = (grad_kf.reshape(TOKENS, FEATURES) * k_feat32).astype(jnp.bfloat16)
        grad_q = lax.dot_general(query_terms, omega, (((1,), (1,)), ((), ())), preferred_element_type=jnp.float32) * feat_scale
        key_total = lax.optimization_barrier(jnp.sum(key_terms.astype(jnp.float32), axis=1, keepdims=True))
        grad_k = lax.dot_general(key_terms, omega, (((1,), (1,)), ((), ())), preferred_element_type=jnp.float32) * feat_scale
        grad_k = grad_k - key_total * k_wide * (feat_scale * feat_scale)
        return (mixed_head, grad_q.astype(jnp.bfloat16), grad_k.astype(jnp.bfloat16), grad_v.reshape(TOKENS, HEAD_DIM).astype(jnp.bfloat16))

    def by_head(matrix):
        return jnp.transpose(matrix.reshape(TOKENS, HEADS, HEAD_DIM), (1, 0, 2))

    def from_heads(stacked):
        return jnp.transpose(stacked, (1, 0, 2)).reshape(TOKENS, HEADS * HEAD_DIM)
    weight_rows = out_weight.reshape(HEADS, HEAD_DIM, DW)
    mixed_all, grad_q_all, grad_k_all, grad_v_all = lax.map(one_head, (by_head(queries), by_head(key_vectors), by_head(value_vectors), feature_proj, weight_rows))
    mixed_flat = from_heads(mixed_all)
    layer_out = jnp.dot(mixed_flat, out_weight, preferred_element_type=jnp.float32).astype(jnp.bfloat16)
    return (layer_out, from_heads(grad_q_all), from_heads(grad_k_all), from_heads(grad_v_all))
```

```python
import functools
import math

import jax
import jax.numpy as jnp
from jax import lax
from jax.experimental import pallas as pl
from jax.experimental.pallas import tpu as pltpu
from jax.sharding import PartitionSpec as P

EPSILON = 1e-05
F32 = jnp.float32
BF16 = jnp.bfloat16
MESH = pl.DeviceIdType.MESH
NN = (((1,), (0,)), ((), ()))
NT = (((1,), (1,)), ((), ()))
TN = (((0,), (0,)), ((), ()))


def mm(a, b, dims):
    return lax.dot_general(a, b, dims, preferred_element_type=F32)


def far_first(n):
    return sorted(range(1, n), key=lambda d: -min(d, n - d))


def kernel(ny, nz, nx, toks, width, feats, *refs):
    (q_in, k_in, v_in, om_in, w_in, g_in,
     lo_out, gq_out, gk_out, gv_out,
     qc, kc, vc, om, w, g_all, gm,
     kf32, kf, qf32, qf, sc, gs, gn, normed, intra, kintra, vintra,
     st, p1, x2, p2, x3, total,
     mixed, mx, po, rs, lo, gq, gk, gv,
     in_sem, pair_send, pair_recv, x_send, x_recv, scan_send, scan_recv, out_sem) = refs
    me = lax.axis_index("seq")
    x = lax.axis_index("head")
    core = lax.rem(me, 2)
    y = lax.rem(lax.div(me, 2), ny)
    z = lax.div(me, 2 * ny)
    span = 2 * width
    slice_rows = feats // ny
    rows = 2 * toks
    own = pl.multiple_of(core * toks, toks)
    other = pl.multiple_of((1 - core) * toks, toks)
    own_cols = pl.multiple_of(core * span, span)
    other_cols = pl.multiple_of((1 - core) * span, span)
    scale = width ** (-0.25)

    def seq_id(zz, yy, cc):
        return {"seq": (zz * ny + yy) * 2 + cc, "head": x}

    partner = seq_id(z, y, 1 - core)
    y_peers = [lax.rem(y + d, ny) for d in far_first(ny)]
    z_peers = [lax.rem(z + d, nz) for d in far_first(nz)]
    x_peers = [lax.rem(x + d, nx) for d in far_first(nx)]

    barrier = pltpu.get_barrier_semaphore()
    peers = [partner]
    peers += [seq_id(z, yy, core) for yy in y_peers]
    peers += [seq_id(zz, y, core) for zz in z_peers]
    peers += [{"seq": me, "head": xx} for xx in x_peers]
    for peer in peers:
        pl.semaphore_signal(barrier, inc=1, device_id=peer, device_id_type=MESH)

    def fetch(src, dst, index):
        copy = pltpu.make_async_copy(src, dst, in_sem.at[index])
        copy.start()
        return copy

    own_col = pl.ds(own_cols, span)
    got_k = fetch(k_in.at[:, own_col], kc.at[pl.ds(own, toks), :], 0)
    got_om = fetch(om_in.at[pl.ds(core * 2, 2)], om, 1)
    got_q = fetch(q_in.at[:, own_col], qc.at[pl.ds(own, toks), :], 2)
    got_v = fetch(v_in.at[:, own_col], vc.at[pl.ds(own, toks), :], 3)
    got_g = fetch(g_in, g_all.at[x], 4)
    got_w = fetch(w_in, w, 5)

    def k_feats(start):
        for h in range(2):
            cols = slice(h * width, (h + 1) * width)
            kb = kc[pl.ds(start, toks), cols]
            wide = kb.astype(F32)
            half = jnp.sum(wide * wide, axis=1, keepdims=True) * (scale * scale * 0.5)
            value = jnp.exp(mm(kb, om[h], NN) * scale - half)
            kf32[h, pl.ds(start, toks), :] = value
            kf[h, pl.ds(start, toks), :] = value.astype(BF16)

    def q_feats(start):
        for h in range(2):
            cols = slice(h * width, (h + 1) * width)
            value = jnp.exp(mm(qc[pl.ds(start, toks), cols], om[h], NN) * scale)
            qf32[h, pl.ds(start, toks), :] = value
            qf[h, pl.ds(start, toks), :] = value.astype(BF16)

    got_k.wait()
    got_om.wait()
    k_feats(own)
    got_q.wait()
    q_feats(own)

    pl.semaphore_wait(barrier, len(peers))

    def to_partner(src, dst, index):
        copy = pltpu.make_async_remote_copy(
            src_ref=src, dst_ref=dst, send_sem=pair_send.at[index], recv_sem=pair_recv.at[index],
            device_id=partner, device_id_type=MESH)
        copy.start()
        return copy

    other_col = pl.ds(other_cols, span)
    own_rows = pl.ds(own, toks)
    other_rows = pl.ds(other, toks)
    sent_k = to_partner(k_in.at[:, other_col], kc.at[own_rows, :], 0)
    sent_v = to_partner(v_in.at[:, other_col], vc.at[own_rows, :], 1)
    sent_q = to_partner(q_in.at[:, other_col], qc.at[own_rows, :], 2)

    sent_g = []
    for i, xx in enumerate(x_peers):
        copy = pltpu.make_async_remote_copy(
            src_ref=g_in, dst_ref=g_all.at[x], send_sem=x_send.at[0], recv_sem=x_recv.at[0],
            device_id={"seq": me, "head": xx}, device_id_type=MESH)
        copy.start()

    got_v.wait()
    sent_k.wait_recv()
    k_feats(other)
    sent_v.wait_recv()

    def all_sent(ref, sem):
        pltpu.make_async_copy(ref, ref, sem).wait()

    class Scan:
        def __init__(self, index, backward):
            self.i, self.backward = index, backward

        def sems(self, phase, h):
            return scan_send.at[self.i, phase, h], scan_recv.at[self.i, phase, h]

        def start(self, h, state):
            i = self.i
            value = state.astype(BF16)
            for s in range(ny):
                st[i, h, s] = value[s * slice_rows:(s + 1) * slice_rows]
            ss, rr = self.sems(0, h)
            for yy in y_peers:
                pltpu.make_async_remote_copy(
                    src_ref=st.at[i, h, yy], dst_ref=p1.at[i, h, y], send_sem=ss, recv_sem=rr,
                    device_id=seq_id(z, yy, core), device_id_type=MESH).start()
            p1[i, h, y] = st[i, h, y]

        def middle(self, h):
            i = self.i
            all_sent(p1.at[i, h, pl.ds(0, ny - 1)], self.sems(0, h)[1])
            order = range(ny)[::-1] if self.backward else range(ny)
            acc = jnp.zeros((slice_rows, width), F32)
            for s in order:
                x3[i, h, s] = acc
                acc = acc + p1[i, h, s].astype(F32)
            x2[i, h] = acc.astype(BF16)
            ss, rr = self.sems(1, h)
            for zz in z_peers:
                pltpu.make_async_remote_copy(
                    src_ref=x2.at[i, h], dst_ref=p2.at[i, h, z], send_sem=ss, recv_sem=rr,
                    device_id=seq_id(zz, y, core), device_id_type=MESH).start()
            p2[i, h, z] = x2[i, h]

        def back(self, h):
            i = self.i
            all_sent(p2.at[i, h, pl.ds(0, nz - 1)], self.sems(1, h)[1])
            acc = jnp.zeros((slice_rows, width), F32)
            for s in range(nz):
                take = (s > z) if self.backward else (s < z)
                acc = acc + jnp.where(take, p2[i, h, s].astype(F32), 0.0)
            for s in range(ny):
                st[2 + i, h, s] = (x3[i, h, s] + acc).astype(BF16)
            ss, rr = self.sems(2, h)
            for yy in y_peers:
                pltpu.make_async_remote_copy(
                    src_ref=st.at[2 + i, h, yy], dst_ref=total.at[i, h, y], send_sem=ss, recv_sem=rr,
                    device_id=seq_id(z, yy, core), device_id_type=MESH).start()
            total[i, h, y] = st[2 + i, h, y]

        def result(self, h):
            i = self.i
            all_sent(total.at[i, h, pl.ds(0, ny - 1)], self.sems(2, h)[1])
            return total[i, h].reshape(feats, width)

        def finish(self):
            i = self.i
            for h in range(2):
                all_sent(p1.at[i, h, pl.ds(0, ny - 1)], self.sems(0, h)[0])
                all_sent(p2.at[i, h, pl.ds(0, nz - 1)], self.sems(1, h)[0])
                all_sent(total.at[i, h, pl.ds(0, ny - 1)], self.sems(2, h)[0])

    causal = (lax.broadcasted_iota(jnp.int32, (rows, rows), 1)
              <= lax.broadcasted_iota(jnp.int32, (rows, rows), 0))
    head_cols = [slice(h * width, (h + 1) * width) for h in range(2)]

    forward = Scan(0, False)
    for h in range(2):
        forward.start(h, mm(kf[h], vc[:, head_cols[h]], TN))

    sent_q.wait_recv()
    q_feats(other)
    for h in range(2):
        forward.middle(h)

    for h in range(2):
        scores = jnp.where(causal, mm(qf[h], kf[h], NT), 0.0).astype(BF16)
        sc[h] = scores
        intra[h] = mm(scores, vc[:, head_cols[h]], NN)
    for h in range(2):
        forward.back(h)

    got_g.wait()
    got_w.wait()
    all_sent(g_all.at[pl.ds(0, nx - 1)], x_recv.at[0])
    block = g_in.shape[1]
    grad = mm(g_all[0], w[:, 0:block], NT)
    for s in range(1, nx):
        grad = grad + mm(g_all[s], w[:, s * block:(s + 1) * block], NT)
    for c in range(2):
        gm[2 + c] = grad[:, c * span:(c + 1) * span]
    gm[core] = gm[2 + core]
    sent_gm = to_partner(gm.at[3 - core], gm.at[core], 3)
    sent_gm.wait_recv()

    backward = Scan(1, True)
    for h in range(2):
        carried = forward.result(h)
        numer = intra[h] + mm(qf[h], carried, NN)
        root = jnp.sqrt(jnp.mean(numer * numer, axis=1, keepdims=True) + EPSILON)
        unit = numer / root
        normed[h] = unit
        grad = jnp.concatenate([gm[0, :, head_cols[h]], gm[1, :, head_cols[h]]], axis=0)
        grad = (grad - unit * jnp.mean(grad * unit, axis=1, keepdims=True)) / root
        grad = grad.astype(BF16)
        gn[h] = grad
        backward.start(h, mm(qf[h], grad, TN))

    for h in range(2):
        mixed[:, head_cols[h]] = normed[h].astype(BF16)
    mx[:, own_col] = mixed[own_rows, :]
    sent_mx = to_partner(mixed.at[other_rows, :], mx.at[:, own_col], 4)

    for h in range(2):
        grad_scores = jnp.where(causal, mm(gn[h], vc[:, head_cols[h]], NT), 0.0).astype(BF16)
        gs[h] = grad_scores
    for h in range(2):
        backward.middle(h)

    sent_mx.wait_recv()
    for s in range(nx):
        po[s] = mm(mx[...], w[:, s * block:(s + 1) * block], NN).astype(BF16)
    for xx in x_peers:
        pltpu.make_async_remote_copy(
            src_ref=po.at[xx], dst_ref=rs.at[x], send_sem=x_send.at[1], recv_sem=x_recv.at[1],
            device_id={"seq": me, "head": xx}, device_id_type=MESH).start()
    rs[x] = po[x]
    for h in range(2):
        backward.back(h)

    def deliver(staged, out, index):
        keep = pltpu.make_async_copy(
            staged.at[own_rows, :], out.at[:, own_col], out_sem.at[index])
        keep.start()
        return keep, to_partner(staged.at[other_rows, :], out.at[:, own_col], 4 + index)

    for h in range(2):
        carried = total[0, h].reshape(feats, width)
        grad_qf = mm(gs[h], kf[h], NN) + mm(gn[h], carried, NT)
        terms = (grad_qf * qf32[h]).astype(BF16)
        gq[:, head_cols[h]] = (mm(terms, om[h], NT) * scale).astype(BF16)
        kintra[h] = mm(gs[h], qf[h], TN)
        vintra[h] = mm(sc[h], gn[h], TN)
    pending = [deliver(gq, gq_out, 1)]

    all_sent(rs.at[pl.ds(0, nx - 1)], x_recv.at[1])
    layer = rs[0].astype(F32)
    for s in range(1, nx):
        layer = layer + rs[s].astype(F32)
    lo[...] = layer.astype(BF16)
    lo_copy = pltpu.make_async_copy(lo, lo_out, out_sem.at[0])
    lo_copy.start()

    for h in range(2):
        after = backward.result(h)
        gv[:, head_cols[h]] = (vintra[h] + mm(kf[h], after, NN)).astype(BF16)
        grad_kf = kintra[h] + mm(vc[:, head_cols[h]], after, NT)
        terms = (grad_kf * kf32[h]).astype(BF16)
        key_total = jnp.sum(terms.astype(F32), axis=1, keepdims=True)
        grad = mm(terms, om[h], NT) * scale
        grad = grad - key_total * kc[:, head_cols[h]].astype(F32) * (scale * scale)
        gk[:, head_cols[h]] = grad.astype(BF16)
    pending.append(deliver(gv, gv_out, 2))
    pending.append(deliver(gk, gk_out, 3))

    for copy in (sent_k, sent_v, sent_q, sent_gm, sent_mx):
        copy.wait_send()
    for i in range(2):
        all_sent(rs.at[pl.ds(0, nx - 1)], x_send.at[i])
    forward.finish()
    backward.finish()
    lo_copy.wait()
    for keep, sent in pending:
        keep.wait()
        sent.wait()


def local(queries, key_vectors, value_vectors, feature_proj, out_weight, grad_output):
    toks, cols = queries.shape
    width, feats = feature_proj.shape[1:]
    nx = lax.axis_size("head")
    ny = math.isqrt(lax.axis_size("seq") // 2)
    nz = lax.axis_size("seq") // (2 * ny)
    rows, span = 2 * toks, 2 * width
    part = feats // ny
    vm = pltpu.VMEM
    scratch = [
        vm((rows, span), BF16), vm((rows, span), BF16), vm((rows, span), BF16),
        vm((2, width, feats), BF16), vm(out_weight.shape, BF16),
        vm((nx, toks, cols), BF16), vm((4, toks, span), F32),
        vm((2, rows, feats), F32), vm((2, rows, feats), BF16),
        vm((2, rows, feats), F32), vm((2, rows, feats), BF16),
        vm((2, rows, rows), BF16), vm((2, rows, rows), BF16),
        vm((2, rows, width), BF16), vm((2, rows, width), F32),
        vm((2, rows, width), F32), vm((2, rows, feats), F32),
        vm((2, rows, width), F32),
        vm((4, 2, ny, part, width), BF16), vm((2, 2, ny, part, width), BF16),
        vm((2, 2, part, width), BF16), vm((2, 2, nz, part, width), BF16),
        vm((2, 2, ny, part, width), F32), vm((2, 2, ny, part, width), BF16),
        vm((rows, span), BF16), vm((toks, cols), BF16),
        vm((nx, toks, cols), BF16), vm((nx, toks, cols), BF16),
        vm((toks, cols), BF16), vm((rows, span), BF16),
        vm((rows, span), BF16), vm((rows, span), BF16),
        pltpu.SemaphoreType.DMA((6,)), pltpu.SemaphoreType.DMA((8,)),
        pltpu.SemaphoreType.DMA((8,)), pltpu.SemaphoreType.DMA((2,)),
        pltpu.SemaphoreType.DMA((2,)), pltpu.SemaphoreType.DMA((2, 3, 2)),
        pltpu.SemaphoreType.DMA((2, 3, 2)), pltpu.SemaphoreType.DMA((4,)),
    ]
    out = jax.ShapeDtypeStruct((toks, cols), BF16)
    return pl.pallas_call(
        functools.partial(kernel, ny, nz, nx, toks, width, feats),
        out_shape=(out,) * 4,
        in_specs=[pl.BlockSpec(memory_space=pl.ANY)] * 6,
        out_specs=(pl.BlockSpec(memory_space=pl.ANY),) * 4,
        scratch_shapes=scratch,
        compiler_params=pltpu.CompilerParams(collective_id=0, has_side_effects=True),
    )(queries, key_vectors, value_vectors, feature_proj, out_weight, grad_output)


def solution(mesh):
    rows = P("seq", "head")
    return jax.shard_map(
        local,
        mesh=mesh,
        in_specs=(rows, rows, rows, P("head", None, None), P("head", None), rows),
        out_specs=(rows,) * 4,
        check_vma=False,
    )
```

```python
import functools
import math

import jax
import jax.numpy as jnp
from jax import lax
from jax.experimental import pallas as pl
from jax.experimental.pallas import tpu as pltpu
from jax.sharding import PartitionSpec as P

EPSILON = 1e-05
F32 = jnp.float32
BF16 = jnp.bfloat16
MESH = pl.DeviceIdType.MESH
NN = (((1,), (0,)), ((), ()))
NT = (((1,), (1,)), ((), ()))
TN = (((0,), (0,)), ((), ()))


def mm(a, b, dims):
    return lax.dot_general(a, b, dims, preferred_element_type=F32)


def far_first(n):
    return sorted(range(1, n), key=lambda d: -min(d, n - d))


def kernel(ny, nz, nx, toks, width, feats, *refs):
    (q_in, k_in, v_in, om_in, w_in, g_in,
     lo_out, gq_out, gk_out, gv_out,
     qc, kc, vc, om, w, g_all, gm,
     kf32, kf, qf32, qf, sc, gs, gn, normed, intra, kintra, vintra,
     st, p1, x2, p2, x3, total,
     mixed, mx, po, rs, gq, gk, gv,
     in_sem, pair_send, pair_recv, x_send, x_recv, scan_send, scan_recv, out_sem) = refs
    me = lax.axis_index("seq")
    x = lax.axis_index("head")
    core = lax.rem(me, 2)
    y = lax.rem(lax.div(me, 2), ny)
    z = lax.div(me, 2 * ny)
    span = 2 * width
    slice_rows = feats // ny
    rows = 2 * toks
    own = pl.multiple_of(core * toks, toks)
    other = pl.multiple_of((1 - core) * toks, toks)
    own_cols = pl.multiple_of(core * span, span)
    other_cols = pl.multiple_of((1 - core) * span, span)
    scale = width ** (-0.25)

    def seq_id(zz, yy, cc):
        return {"seq": (zz * ny + yy) * 2 + cc, "head": x}

    partner = seq_id(z, y, 1 - core)
    y_peers = [lax.rem(y + d, ny) for d in far_first(ny)]
    z_peers = [lax.rem(z + d, nz) for d in far_first(nz)]
    x_peers = [lax.rem(x + d, nx) for d in far_first(nx)]

    barrier = pltpu.get_barrier_semaphore()
    peers = [partner]
    peers += [seq_id(z, yy, core) for yy in y_peers]
    peers += [seq_id(zz, y, core) for zz in z_peers]
    peers += [{"seq": me, "head": xx} for xx in x_peers]
    for peer in peers:
        pl.semaphore_signal(barrier, inc=1, device_id=peer, device_id_type=MESH)

    def fetch(src, dst, index):
        copy = pltpu.make_async_copy(src, dst, in_sem.at[index])
        copy.start()
        return copy

    own_col = pl.ds(own_cols, span)
    got_k = fetch(k_in.at[:, own_col], kc.at[pl.ds(own, toks), :], 0)
    got_om = fetch(om_in.at[pl.ds(core * 2, 2)], om, 1)
    got_q = fetch(q_in.at[:, own_col], qc.at[pl.ds(own, toks), :], 2)
    got_v = fetch(v_in.at[:, own_col], vc.at[pl.ds(own, toks), :], 3)
    got_g = fetch(g_in, g_all.at[x], 4)
    got_w = fetch(w_in, w, 5)

    def k_feats(start):
        for h in range(2):
            cols = slice(h * width, (h + 1) * width)
            kb = kc[pl.ds(start, toks), cols]
            wide = kb.astype(F32)
            half = jnp.sum(wide * wide, axis=1, keepdims=True) * (scale * scale * 0.5)
            value = jnp.exp(mm(kb, om[h], NN) * scale - half)
            kf32[h, pl.ds(start, toks), :] = value
            kf[h, pl.ds(start, toks), :] = value.astype(BF16)

    def q_feats(start):
        for h in range(2):
            cols = slice(h * width, (h + 1) * width)
            value = jnp.exp(mm(qc[pl.ds(start, toks), cols], om[h], NN) * scale)
            qf32[h, pl.ds(start, toks), :] = value
            qf[h, pl.ds(start, toks), :] = value.astype(BF16)

    got_k.wait()
    got_om.wait()
    k_feats(own)
    got_q.wait()
    q_feats(own)

    pl.semaphore_wait(barrier, len(peers))

    def to_partner(src, dst, index):
        copy = pltpu.make_async_remote_copy(
            src_ref=src, dst_ref=dst, send_sem=pair_send.at[index], recv_sem=pair_recv.at[index],
            device_id=partner, device_id_type=MESH)
        copy.start()
        return copy

    other_col = pl.ds(other_cols, span)
    own_rows = pl.ds(own, toks)
    other_rows = pl.ds(other, toks)
    sent_k = to_partner(k_in.at[:, other_col], kc.at[own_rows, :], 0)
    sent_v = to_partner(v_in.at[:, other_col], vc.at[own_rows, :], 1)
    sent_q = to_partner(q_in.at[:, other_col], qc.at[own_rows, :], 2)

    sent_g = []
    for i, xx in enumerate(x_peers):
        copy = pltpu.make_async_remote_copy(
            src_ref=g_in, dst_ref=g_all.at[x], send_sem=x_send.at[0], recv_sem=x_recv.at[0],
            device_id={"seq": me, "head": xx}, device_id_type=MESH)
        copy.start()

    got_v.wait()
    sent_k.wait_recv()
    k_feats(other)
    sent_v.wait_recv()

    def all_sent(ref, sem):
        pltpu.make_async_copy(ref, ref, sem).wait()

    class Scan:
        def __init__(self, index, backward):
            self.i, self.backward = index, backward

        def sems(self, phase, h):
            return scan_send.at[self.i, phase, h], scan_recv.at[self.i, phase, h]

        def start(self, h, state):
            i = self.i
            value = state.astype(BF16)
            for s in range(ny):
                st[i, h, s] = value[s * slice_rows:(s + 1) * slice_rows]
            ss, rr = self.sems(0, h)
            for yy in y_peers:
                pltpu.make_async_remote_copy(
                    src_ref=st.at[i, h, yy], dst_ref=p1.at[i, h, y], send_sem=ss, recv_sem=rr,
                    device_id=seq_id(z, yy, core), device_id_type=MESH).start()
            p1[i, h, y] = st[i, h, y]

        def middle(self, h):
            i = self.i
            all_sent(p1.at[i, h, pl.ds(0, ny - 1)], self.sems(0, h)[1])
            order = range(ny)[::-1] if self.backward else range(ny)
            acc = jnp.zeros((slice_rows, width), F32)
            for s in order:
                x3[i, h, s] = acc
                acc = acc + p1[i, h, s].astype(F32)
            x2[i, h] = acc.astype(BF16)
            ss, rr = self.sems(1, h)
            for zz in z_peers:
                pltpu.make_async_remote_copy(
                    src_ref=x2.at[i, h], dst_ref=p2.at[i, h, z], send_sem=ss, recv_sem=rr,
                    device_id=seq_id(zz, y, core), device_id_type=MESH).start()
            p2[i, h, z] = x2[i, h]

        def back(self, h):
            i = self.i
            all_sent(p2.at[i, h, pl.ds(0, nz - 1)], self.sems(1, h)[1])
            acc = jnp.zeros((slice_rows, width), F32)
            for s in range(nz):
                take = (s > z) if self.backward else (s < z)
                acc = acc + jnp.where(take, p2[i, h, s].astype(F32), 0.0)
            for s in range(ny):
                st[2 + i, h, s] = (x3[i, h, s] + acc).astype(BF16)
            ss, rr = self.sems(2, h)
            for yy in y_peers:
                pltpu.make_async_remote_copy(
                    src_ref=st.at[2 + i, h, yy], dst_ref=total.at[i, h, y], send_sem=ss, recv_sem=rr,
                    device_id=seq_id(z, yy, core), device_id_type=MESH).start()
            total[i, h, y] = st[2 + i, h, y]

        def result(self, h):
            i = self.i
            all_sent(total.at[i, h, pl.ds(0, ny - 1)], self.sems(2, h)[1])
            return total[i, h].reshape(feats, width)

        def finish(self):
            i = self.i
            for h in range(2):
                all_sent(p1.at[i, h, pl.ds(0, ny - 1)], self.sems(0, h)[0])
                all_sent(p2.at[i, h, pl.ds(0, nz - 1)], self.sems(1, h)[0])
                all_sent(total.at[i, h, pl.ds(0, ny - 1)], self.sems(2, h)[0])

    causal = (lax.broadcasted_iota(jnp.int32, (rows, rows), 1)
              <= lax.broadcasted_iota(jnp.int32, (rows, rows), 0))
    head_cols = [slice(h * width, (h + 1) * width) for h in range(2)]

    forward = Scan(0, False)
    for h in range(2):
        forward.start(h, mm(kf[h], vc[:, head_cols[h]], TN))

    sent_q.wait_recv()
    q_feats(other)
    for h in range(2):
        forward.middle(h)

    for h in range(2):
        scores = jnp.where(causal, mm(qf[h], kf[h], NT), 0.0).astype(BF16)
        sc[h] = scores
        intra[h] = mm(scores, vc[:, head_cols[h]], NN)
    for h in range(2):
        forward.back(h)

    got_g.wait()
    got_w.wait()
    all_sent(g_all.at[pl.ds(0, nx - 1)], x_recv.at[0])
    block = g_in.shape[1]
    grad = mm(g_all[0], w[:, 0:block], NT)
    for s in range(1, nx):
        grad = grad + mm(g_all[s], w[:, s * block:(s + 1) * block], NT)
    for c in range(2):
        gm[2 + c] = grad[:, c * span:(c + 1) * span]
    gm[core] = gm[2 + core]
    sent_gm = to_partner(gm.at[3 - core], gm.at[core], 3)
    sent_gm.wait_recv()

    backward = Scan(1, True)
    for h in range(2):
        carried = forward.result(h)
        numer = intra[h] + mm(qf[h], carried, NN)
        root = jnp.sqrt(jnp.mean(numer * numer, axis=1, keepdims=True) + EPSILON)
        unit = numer / root
        normed[h] = unit
        grad = jnp.concatenate([gm[0, :, head_cols[h]], gm[1, :, head_cols[h]]], axis=0)
        grad = (grad - unit * jnp.mean(grad * unit, axis=1, keepdims=True)) / root
        grad = grad.astype(BF16)
        gn[h] = grad
        backward.start(h, mm(qf[h], grad, TN))

    for h in range(2):
        mixed[:, head_cols[h]] = normed[h].astype(BF16)
    mx[:, own_col] = mixed[own_rows, :]
    sent_mx = to_partner(mixed.at[other_rows, :], mx.at[:, own_col], 4)

    for h in range(2):
        grad_scores = jnp.where(causal, mm(gn[h], vc[:, head_cols[h]], NT), 0.0).astype(BF16)
        gs[h] = grad_scores
    for h in range(2):
        backward.middle(h)

    sent_mx.wait_recv()
    for s in range(nx):
        po[s] = mm(mx[...], w[:, s * block:(s + 1) * block], NN).astype(BF16)
    for xx in x_peers:
        pltpu.make_async_remote_copy(
            src_ref=po.at[xx], dst_ref=rs.at[x], send_sem=x_send.at[1], recv_sem=x_recv.at[1],
            device_id={"seq": me, "head": xx}, device_id_type=MESH).start()
    rs[x] = po[x]
    for h in range(2):
        backward.back(h)

    def deliver(staged, out, index):
        keep = pltpu.make_async_copy(
            staged.at[own_rows, :], out.at[:, own_col], out_sem.at[index])
        keep.start()
        return keep, to_partner(staged.at[other_rows, :], out.at[:, own_col], 4 + index)

    for h in range(2):
        carried = total[0, h].reshape(feats, width)
        grad_qf = mm(gs[h], kf[h], NN) + mm(gn[h], carried, NT)
        terms = (grad_qf * qf32[h]).astype(BF16)
        gq[:, head_cols[h]] = (mm(terms, om[h], NT) * scale).astype(BF16)
        kintra[h] = mm(gs[h], qf[h], TN)
        vintra[h] = mm(sc[h], gn[h], TN)
    pending = [deliver(gq, gq_out, 1)]

    all_sent(rs.at[pl.ds(0, nx - 1)], x_recv.at[1])
    layer = rs[0].astype(F32)
    for s in range(1, nx):
        layer = layer + rs[s].astype(F32)
    lo_out[...] = layer.astype(BF16)

    for h in range(2):
        after = backward.result(h)
        gv[:, head_cols[h]] = (vintra[h] + mm(kf[h], after, NN)).astype(BF16)
        grad_kf = kintra[h] + mm(vc[:, head_cols[h]], after, NT)
        terms = (grad_kf * kf32[h]).astype(BF16)
        key_total = jnp.sum(terms.astype(F32), axis=1, keepdims=True)
        grad = mm(terms, om[h], NT) * scale
        grad = grad - key_total * kc[:, head_cols[h]].astype(F32) * (scale * scale)
        gk[:, head_cols[h]] = grad.astype(BF16)
    pending.append(deliver(gv, gv_out, 2))
    pending.append(deliver(gk, gk_out, 3))

    for copy in (sent_k, sent_v, sent_q, sent_gm, sent_mx):
        copy.wait_send()
    for i in range(2):
        all_sent(rs.at[pl.ds(0, nx - 1)], x_send.at[i])
    forward.finish()
    backward.finish()
    for keep, sent in pending:
        keep.wait()
        sent.wait()


def write_out(*refs):
    copies = [pltpu.make_async_copy(refs[i], refs[4 + i], refs[8].at[i]) for i in range(4)]
    for copy in copies:
        copy.start()
    for copy in copies:
        copy.wait()


def local(queries, key_vectors, value_vectors, feature_proj, out_weight, grad_output):
    toks, cols = queries.shape
    width, feats = feature_proj.shape[1:]
    nx = lax.axis_size("head")
    ny = math.isqrt(lax.axis_size("seq") // 2)
    nz = lax.axis_size("seq") // (2 * ny)
    rows, span = 2 * toks, 2 * width
    part = feats // ny
    vm = pltpu.VMEM
    scratch = [
        vm((rows, span), BF16), vm((rows, span), BF16), vm((rows, span), BF16),
        vm((2, width, feats), BF16), vm(out_weight.shape, BF16),
        vm((nx, toks, cols), BF16), vm((4, toks, span), F32),
        vm((2, rows, feats), F32), vm((2, rows, feats), BF16),
        vm((2, rows, feats), F32), vm((2, rows, feats), BF16),
        vm((2, rows, rows), BF16), vm((2, rows, rows), BF16),
        vm((2, rows, width), BF16), vm((2, rows, width), F32),
        vm((2, rows, width), F32), vm((2, rows, feats), F32),
        vm((2, rows, width), F32),
        vm((4, 2, ny, part, width), BF16), vm((2, 2, ny, part, width), BF16),
        vm((2, 2, part, width), BF16), vm((2, 2, nz, part, width), BF16),
        vm((2, 2, ny, part, width), F32), vm((2, 2, ny, part, width), BF16),
        vm((rows, span), BF16), vm((toks, cols), BF16),
        vm((nx, toks, cols), BF16), vm((nx, toks, cols), BF16),
        vm((rows, span), BF16), vm((rows, span), BF16), vm((rows, span), BF16),
        pltpu.SemaphoreType.DMA((6,)), pltpu.SemaphoreType.DMA((8,)),
        pltpu.SemaphoreType.DMA((8,)), pltpu.SemaphoreType.DMA((2,)),
        pltpu.SemaphoreType.DMA((2,)), pltpu.SemaphoreType.DMA((2, 3, 2)),
        pltpu.SemaphoreType.DMA((2, 3, 2)), pltpu.SemaphoreType.DMA((4,)),
    ]
    out = jax.ShapeDtypeStruct((toks, cols), BF16)
    held = pltpu.VMEM((toks, cols), BF16)
    staged = pl.pallas_call(
        functools.partial(kernel, ny, nz, nx, toks, width, feats),
        out_shape=(held,) * 4,
        in_specs=[pl.BlockSpec(memory_space=pl.ANY)] * 6,
        out_specs=(pl.BlockSpec(memory_space=pltpu.VMEM),) * 4,
        scratch_shapes=scratch,
        compiler_params=pltpu.CompilerParams(collective_id=0, has_side_effects=True),
    )(queries, key_vectors, value_vectors, feature_proj, out_weight, grad_output)
    return pl.pallas_call(
        write_out,
        out_shape=(out,) * 4,
        in_specs=[pl.BlockSpec(memory_space=pl.ANY)] * 4,
        compiler_params=pltpu.CompilerParams(vmem_limit_bytes=1 << 20),
        out_specs=(pl.BlockSpec(memory_space=pl.ANY),) * 4,
        scratch_shapes=[pltpu.SemaphoreType.DMA((4,))],
    )(*staged)


def solution(mesh):
    rows = P("seq", "head")
    return jax.shard_map(
        local,
        mesh=mesh,
        in_specs=(rows, rows, rows, P("head", None, None), P("head", None), rows),
        out_specs=(rows,) * 4,
        check_vma=False,
    )
```

```python
import functools
import itertools
import math

import jax
import jax.numpy as jnp
from jax import lax
from jax.experimental import pallas as pl
from jax.experimental.pallas import tpu as pltpu
from jax.sharding import PartitionSpec as P

EPSILON = 1e-05
F32 = jnp.float32
BF16 = jnp.bfloat16
MESH = pl.DeviceIdType.MESH
NN = (((1,), (0,)), ((), ()))
NT = (((1,), (1,)), ((), ()))
TN = (((0,), (0,)), ((), ()))


def mm(a, b, dims):
    return lax.dot_general(a, b, dims, preferred_element_type=F32)


def far_first(n):
    return sorted(range(1, n), key=lambda d: -min(d, n - d))


def kernel(ny, nz, nx, toks, width, feats, *refs):
    (q_in, k_in, v_in, om_in, w_in, g_in,
     lo_out, gq_out, gk_out, gv_out,
     qc, kc, vc, ko, vo, om, omo, w, g_all, gm,
     kf32, kf, qf32, qf, sc, gs, gn, normed, intra, kintra, vintra,
     st, p1, x2, p2, x3, total,
     mixed, mx, po, rs, gq, gk, gv, mine, away, got, qft, omt,
     direct, pd, pf, tother, kfo, kfo32, kio, vio, omto,
     in_sem, pair_send, pair_recv, x_send, x_recv, scan_send, scan_recv, both_sem) = refs
    me = lax.axis_index("seq")
    x = lax.axis_index("head")
    core = lax.rem(me, 2)
    y = lax.rem(lax.div(me, 2), ny)
    z = lax.div(me, 2 * ny)
    span = 2 * width
    slice_rows = feats // ny
    rows = 2 * toks
    own = pl.multiple_of(core * toks, toks)
    other = pl.multiple_of((1 - core) * toks, toks)
    own_cols = pl.multiple_of(core * span, span)
    other_cols = pl.multiple_of((1 - core) * span, span)
    scale = width ** (-0.25)

    def seq_id(zz, yy, cc):
        return {"seq": (zz * ny + yy) * 2 + cc, "head": x}

    partner = seq_id(z, y, 1 - core)
    y_peers = [lax.rem(y + d, ny) for d in far_first(ny)]
    z_peers = [lax.rem(z + d, nz) for d in far_first(nz)]
    x_peers = [lax.rem(x + d, nx) for d in far_first(nx)]

    barrier = pltpu.get_barrier_semaphore()
    peers = []
    for yy, zz in itertools.zip_longest(y_peers, z_peers):
        if yy is not None:
            peers.append(seq_id(z, yy, core))
            peers.append(seq_id(z, yy, 1 - core))
        if zz is not None:
            peers.append(seq_id(zz, y, core))
    peers += [{"seq": me, "head": xx} for xx in x_peers] + [partner]
    for peer in peers:
        pl.semaphore_signal(barrier, inc=1, device_id=peer, device_id_type=MESH)

    def fetch(src, dst, index):
        copy = pltpu.make_async_copy(src, dst, in_sem.at[index])
        copy.start()
        return copy

    own_col = pl.ds(own_cols, span)
    got_k = fetch(k_in.at[:, own_col], kc.at[pl.ds(own, toks), :], 0)
    got_om = fetch(om_in.at[pl.ds(core * 2, 2)], om, 1)
    got_q = fetch(q_in.at[:, own_col], qc.at[pl.ds(own, toks), :], 2)
    got_v = fetch(v_in.at[:, own_col], vc.at[pl.ds(own, toks), :], 3)
    other_col = pl.ds(other_cols, span)
    got_ko = fetch(k_in.at[:, other_col], ko, 6)
    got_omo = fetch(om_in.at[pl.ds((1 - core) * 2, 2)], omo, 7)
    got_vo = fetch(v_in.at[:, other_col], vo, 8)
    got_g = fetch(g_in, g_all.at[x], 4)
    got_w = fetch(w_in, w, 5)

    def key_feature(kb, omega):
        wide = kb.astype(F32)
        half = jnp.sum(wide * wide, axis=1, keepdims=True) * (scale * scale * 0.5)
        return jnp.exp(mm(kb, omega, NN) * scale - half)

    def k_feats(start):
        for h in range(2):
            value = key_feature(kc[pl.ds(start, toks), h * width:(h + 1) * width], om[h])
            kf32[h, pl.ds(start, toks), :] = value
            kf[h, pl.ds(start, toks), :] = value.astype(BF16)

    def q_feats(start):
        for h in range(2):
            cols = slice(h * width, (h + 1) * width)
            value = jnp.exp(mm(qc[pl.ds(start, toks), cols], om[h], NN) * scale)
            qf32[h, pl.ds(start, toks), :] = value
            qf[h, pl.ds(start, toks), :] = value.astype(BF16)

    def put_slices(ref, index, state):
        value = state.astype(BF16)
        for s in range(ny):
            ref[index, s] = value[s * slice_rows:(s + 1) * slice_rows]

    got_k.wait()
    got_om.wait()
    k_feats(own)
    got_v.wait()
    own_rows = pl.ds(own, toks)
    other_rows = pl.ds(other, toks)
    head_cols = [slice(h * width, (h + 1) * width) for h in range(2)]
    got_ko.wait()
    got_omo.wait()
    got_vo.wait()
    for h in range(2):
        feature = key_feature(ko[:, head_cols[h]], omo[h])
        if h == 1:
            kfo32[...] = feature
        feature = feature.astype(BF16)
        if h == 0:
            put_slices(direct, 1 - core, mm(feature, vo[:, head_cols[h]], TN))
        else:
            kfo[...] = feature
            away[...] = mm(feature, vo[:, head_cols[h]], TN).astype(BF16)
    put_slices(direct, core, mm(kf[0, own_rows, :], vc[own_rows, head_cols[0]], TN))
    mine[...] = mm(kf[1, own_rows, :], vc[own_rows, head_cols[1]], TN)
    pl.semaphore_wait(barrier, len(peers))

    def to_partner(src, dst, index):
        copy = pltpu.make_async_remote_copy(
            src_ref=src, dst_ref=dst, send_sem=pair_send.at[index], recv_sem=pair_recv.at[index],
            device_id=partner, device_id_type=MESH)
        copy.start()
        return copy

    sent_away = to_partner(away, got, 0)
    def all_sent(ref, sem):
        pltpu.make_async_copy(ref, ref, sem).wait()

    class Scan:
        def __init__(self, index, backward):
            self.i, self.backward = index, backward

        def sems(self, phase, h):
            return scan_send.at[self.i, phase, h], scan_recv.at[self.i, phase, h]

        def start(self, h, state):
            i = self.i
            put_slices(st.at[i], h, state)
            ss, rr = self.sems(0, h)
            for yy in y_peers:
                pltpu.make_async_remote_copy(
                    src_ref=st.at[i, h, yy], dst_ref=p1.at[i, h, y], send_sem=ss, recv_sem=rr,
                    device_id=seq_id(z, yy, core), device_id_type=MESH).start()
            p1[i, h, y] = st[i, h, y]

        def start_direct(self):
            ss, rr = self.sems(0, 0)
            for yy in y_peers:
                for cc in (core, 1 - core):
                    pltpu.make_async_remote_copy(
                        src_ref=direct.at[cc, yy], dst_ref=pd.at[core * ny + y], send_sem=ss, recv_sem=rr,
                        device_id=seq_id(z, yy, cc), device_id_type=MESH).start()
            pltpu.make_async_remote_copy(
                src_ref=direct.at[1 - core, y], dst_ref=pd.at[core * ny + y], send_sem=ss, recv_sem=rr,
                device_id=partner, device_id_type=MESH).start()
            pd[core * ny + y] = direct[core, y]

        def merge(self):
            ss, rr = self.sems(0, 0)
            all_sent(pd.at[pl.ds(0, 2 * ny - 1)], rr)
            for s in range(ny):
                pf[s] = pd[s].astype(F32) + pd[ny + s].astype(F32)

        def middle(self, h):
            i = self.i
            swapped = (i, h) == (0, 0)
            if swapped:
                self.merge()
            else:
                all_sent(p1.at[i, h, pl.ds(0, ny - 1)], self.sems(0, h)[1])

            def term(s):
                return pf[s] if swapped else p1[i, h, s].astype(F32)

            acc = term(0)
            for s in range(1, ny):
                acc = acc + term(s)
            x2[i, h] = acc.astype(BF16)
            ss, rr = self.sems(1, h)
            for zz in z_peers:
                pltpu.make_async_remote_copy(
                    src_ref=x2.at[i, h], dst_ref=p2.at[i, h, z], send_sem=ss, recv_sem=rr,
                    device_id=seq_id(zz, y, core), device_id_type=MESH).start()
            p2[i, h, z] = x2[i, h]
            order = range(ny)[::-1] if self.backward else range(ny)
            acc = jnp.zeros((slice_rows, width), F32)
            for s in order:
                x3[i, h, s] = acc
                acc = acc + term(s)

        def back(self, h):
            i = self.i
            all_sent(p2.at[i, h, pl.ds(0, nz - 1)], self.sems(1, h)[1])
            acc = jnp.zeros((slice_rows, width), F32)
            for s in range(nz):
                take = (s > z) if self.backward else (s < z)
                acc = acc + jnp.where(take, p2[i, h, s].astype(F32), 0.0)
            ss, rr = self.sems(2, h)
            for yy in y_peers:
                st[2 + i, h, yy] = (x3[i, h, yy] + acc).astype(BF16)
                pltpu.make_async_remote_copy(
                    src_ref=st.at[2 + i, h, yy], dst_ref=total.at[i, h, y], send_sem=ss, recv_sem=rr,
                    device_id=seq_id(z, yy, core), device_id_type=MESH).start()
                if (i, h) == (1, 1):
                    self.both(seq_id(z, yy, 1 - core), yy)
            st[2 + i, h, y] = (x3[i, h, y] + acc).astype(BF16)
            total[i, h, y] = st[2 + i, h, y]
            if (i, h) == (1, 1):
                self.both(partner, y)

        def both(self, device, yy):
            pltpu.make_async_remote_copy(
                src_ref=st.at[3, 1, yy], dst_ref=tother.at[y], send_sem=both_sem.at[0],
                recv_sem=both_sem.at[1], device_id=device, device_id_type=MESH).start()

        def result(self, h):
            i = self.i
            all_sent(total.at[i, h, pl.ds(0, ny - 1)], self.sems(2, h)[1])
            return total[i, h].reshape(feats, width)

        def finish(self):
            i = self.i
            for h in range(2):
                if (i, h) == (0, 0):
                    all_sent(pd.at[pl.ds(0, 2 * ny - 1)], self.sems(0, h)[0])
                else:
                    all_sent(p1.at[i, h, pl.ds(0, ny - 1)], self.sems(0, h)[0])
                all_sent(p2.at[i, h, pl.ds(0, nz - 1)], self.sems(1, h)[0])
                all_sent(total.at[i, h, pl.ds(0, ny - 1)], self.sems(2, h)[0])

    causal = (lax.broadcasted_iota(jnp.int32, (rows, rows), 1)
              <= lax.broadcasted_iota(jnp.int32, (rows, rows), 0))
    forward = Scan(0, False)
    forward.start_direct()
    sent_away.wait_recv()
    forward.start(1, mine[...] + got[...].astype(F32))

    sent_k = to_partner(k_in.at[:, other_col], kc.at[own_rows, :], 2)
    sent_v = to_partner(v_in.at[:, other_col], vc.at[own_rows, :], 3)
    sent_q = to_partner(q_in.at[:, other_col], qc.at[own_rows, :], 4)

    for i, xx in enumerate(x_peers):
        copy = pltpu.make_async_remote_copy(
            src_ref=g_in, dst_ref=g_all.at[x], send_sem=x_send.at[0], recv_sem=x_recv.at[0],
            device_id={"seq": me, "head": xx}, device_id_type=MESH)
        copy.start()

    got_q.wait()
    q_feats(own)
    sent_k.wait_recv()
    k_feats(other)
    sent_q.wait_recv()
    q_feats(other)
    sent_v.wait_recv()
    for h in range(2):
        forward.middle(h)
    for h in range(2):
        qft[h] = qf[h].T
        omt[h] = om[h].T
    omto[...] = omo[1].T

    for h in range(2):
        scores = jnp.where(causal, mm(qf[h], kf[h], NT), 0.0).astype(BF16)
        sc[h] = scores
        intra[h] = mm(scores, vc[:, head_cols[h]], NN)
    for h in range(2):
        forward.back(h)

    got_g.wait()
    got_w.wait()
    all_sent(g_all.at[pl.ds(0, nx - 1)], x_recv.at[0])
    block = g_in.shape[1]
    grad = mm(g_all[0], w[:, 0:block], NT)
    for s in range(1, nx):
        grad = grad + mm(g_all[s], w[:, s * block:(s + 1) * block], NT)
    for c in range(2):
        gm[2 + c] = grad[:, c * span:(c + 1) * span]
    gm[core] = gm[2 + core]
    sent_gm = to_partner(gm.at[3 - core], gm.at[core], 5)
    sent_gm.wait_recv()

    backward = Scan(1, True)
    for h in range(2):
        carried = forward.result(h)
        numer = intra[h] + mm(qf[h], carried, NN)
        root = jnp.sqrt(jnp.mean(numer * numer, axis=1, keepdims=True) + EPSILON)
        unit = numer / root
        normed[h] = unit
        grad = jnp.concatenate([gm[0, :, head_cols[h]], gm[1, :, head_cols[h]]], axis=0)
        grad = (grad - unit * jnp.mean(grad * unit, axis=1, keepdims=True)) / root
        grad = grad.astype(BF16)
        gn[h] = grad
        backward.start(h, mm(qft[h], grad, NN))

    for h in range(2):
        mixed[:, head_cols[h]] = normed[h].astype(BF16)
    mx[:, own_col] = mixed[own_rows, :]
    sent_mx = to_partner(mixed.at[other_rows, :], mx.at[:, own_col], 6)

    for h in range(2):
        grad_scores = jnp.where(causal, mm(gn[h], vc[:, head_cols[h]], NT), 0.0).astype(BF16)
        gs[h] = grad_scores
    for h in range(2):
        backward.middle(h)

    sent_mx.wait_recv()
    for s in range(nx):
        po[s] = mm(mx[...], w[:, s * block:(s + 1) * block], NN).astype(BF16)
    for xx in x_peers:
        pltpu.make_async_remote_copy(
            src_ref=po.at[xx], dst_ref=rs.at[x], send_sem=x_send.at[1], recv_sem=x_recv.at[1],
            device_id={"seq": me, "head": xx}, device_id_type=MESH).start()
    rs[x] = po[x]
    for h in range(2):
        backward.back(h)

    pending = []

    def deliver(staged, out, h, index):
        pending.append(to_partner(staged.at[h, other_rows, :], out.at[core * 2 + h], 7 + 2 * index + h))

    for h in range(2):
        carried = total[0, h].reshape(feats, width)
        grad_qf = mm(gs[h], kf[h], NN) + mm(gn[h], carried, NT)
        terms = (grad_qf * qf32[h]).astype(BF16)
        gq[h] = (mm(terms, om[h], NT) * scale).astype(BF16)
        deliver(gq, gq_out, h, 0)
        gq_out[core * 2 + h] = gq[h, own_rows, :]
        kintra[h] = mm(gs[h], qf[h], TN)
        vintra[h] = mm(sc[h], gn[h], TN)
    sent_intra = [
        to_partner(kintra.at[1, other_rows, :], kio, 10),
        to_partner(vintra.at[1, other_rows, :], vio, 1),
    ]

    all_sent(rs.at[pl.ds(0, nx - 1)], x_recv.at[1])
    layer = rs[0].astype(F32)
    for s in range(1, nx):
        layer = layer + rs[s].astype(F32)
    lo_out[...] = layer.astype(BF16)

    def key_side(value_part, key_part, feature32, feature, values, keys, omega_t, after):
        grad_v = (value_part + mm(feature, after, NN)).astype(BF16)
        grad_kf = key_part + mm(values, after, NT)
        terms = (grad_kf * feature32).astype(BF16)
        key_total = jnp.sum(terms.astype(F32), axis=1, keepdims=True)
        grad = mm(terms, omega_t, NN) * scale
        grad = grad - key_total * keys.astype(F32) * (scale * scale)
        return grad_v, grad.astype(BF16)

    def own_head(h, after, rows):
        return key_side(
            vintra[h, rows, :], kintra[h, rows, :], kf32[h, rows, :], kf[h, rows, :],
            vc[rows, head_cols[h]], kc[rows, head_cols[h]], omt[h], after)

    after = backward.result(0)
    gv[0, other_rows, :], gk[0, other_rows, :] = own_head(0, after, other_rows)
    deliver(gv, gv_out, 0, 1)
    deliver(gk, gk_out, 0, 2)
    gv_out[core * 2], gk_out[core * 2] = own_head(0, after, own_rows)
    after = backward.result(1)
    gv_out[core * 2 + 1], gk_out[core * 2 + 1] = own_head(1, after, own_rows)
    for copy in sent_intra:
        copy.wait_recv()
    all_sent(tother, both_sem.at[1])
    away_head = (1 - core) * 2 + 1
    gv_out[away_head], gk_out[away_head] = key_side(
        vio[...], kio[...], kfo32[...], kfo[...], vo[:, head_cols[1]], ko[:, head_cols[1]],
        omto[...], tother[...].reshape(feats, width))
    all_sent(tother, both_sem.at[0])
    for copy in sent_intra:
        copy.wait_send()

    for copy in (sent_away, sent_k, sent_v, sent_q, sent_gm, sent_mx):
        copy.wait_send()
    for i in range(2):
        all_sent(rs.at[pl.ds(0, nx - 1)], x_send.at[i])
    forward.finish()
    backward.finish()
    for copy in pending:
        copy.wait()


def write_out(heads, width, lo, gq, gk, gv, lo_out, gq_out, gk_out, gv_out, sem):
    copies = [pltpu.make_async_copy(lo, lo_out, sem.at[0])]
    for i, (held, out) in enumerate(((gq, gq_out), (gk, gk_out), (gv, gv_out))):
        for h in range(heads):
            copies.append(pltpu.make_async_copy(
                held.at[h], out.at[:, pl.ds(h * width, width)], sem.at[1 + heads * i + h]))
    for copy in copies:
        copy.start()
    for copy in copies:
        copy.wait()


def local(queries, key_vectors, value_vectors, feature_proj, out_weight, grad_output):
    toks, cols = queries.shape
    width, feats = feature_proj.shape[1:]
    nx = lax.axis_size("head")
    ny = math.isqrt(lax.axis_size("seq") // 2)
    nz = lax.axis_size("seq") // (2 * ny)
    rows, span = 2 * toks, 2 * width
    part = feats // ny
    vm = pltpu.VMEM
    scratch = [
        vm((rows, span), BF16), vm((rows, span), BF16), vm((rows, span), BF16),
        vm((toks, span), BF16), vm((toks, span), BF16),
        vm((2, width, feats), BF16), vm((2, width, feats), BF16),
        vm(out_weight.shape, BF16),
        vm((nx, toks, cols), BF16), vm((4, toks, span), F32),
        vm((2, rows, feats), F32), vm((2, rows, feats), BF16),
        vm((2, rows, feats), F32), vm((2, rows, feats), BF16),
        vm((2, rows, rows), BF16), vm((2, rows, rows), BF16),
        vm((2, rows, width), BF16), vm((2, rows, width), F32),
        vm((2, rows, width), F32), vm((2, rows, feats), F32),
        vm((2, rows, width), F32),
        vm((4, 2, ny, part, width), BF16), vm((2, 2, ny, part, width), BF16),
        vm((2, 2, part, width), BF16), vm((2, 2, nz, part, width), BF16),
        vm((2, 2, ny, part, width), F32), vm((2, 2, ny, part, width), BF16),
        vm((rows, span), BF16), vm((toks, cols), BF16),
        vm((nx, toks, cols), BF16), vm((nx, toks, cols), BF16),
        vm((2, rows, width), BF16), vm((2, rows, width), BF16),
        vm((2, rows, width), BF16), vm((feats, width), F32),
        vm((feats, width), BF16), vm((feats, width), BF16),
        vm((2, feats, rows), BF16), vm((2, feats, width), BF16),
        vm((2, ny, part, width), BF16), vm((2 * ny, part, width), BF16),
        vm((ny, part, width), F32), vm((ny, part, width), BF16),
        vm((toks, feats), BF16), vm((toks, feats), F32),
        vm((toks, feats), F32), vm((toks, width), F32),
        vm((feats, width), BF16),
        pltpu.SemaphoreType.DMA((9,)), pltpu.SemaphoreType.DMA((13,)),
        pltpu.SemaphoreType.DMA((13,)), pltpu.SemaphoreType.DMA((2,)),
        pltpu.SemaphoreType.DMA((2,)), pltpu.SemaphoreType.DMA((2, 3, 2)),
        pltpu.SemaphoreType.DMA((2, 3, 2)), pltpu.SemaphoreType.DMA((2,)),
    ]
    out = jax.ShapeDtypeStruct((toks, cols), BF16)
    heads = cols // width
    flat, by_head = pltpu.VMEM((toks, cols), BF16), pltpu.VMEM((heads, toks, width), BF16)
    staged = pl.pallas_call(
        functools.partial(kernel, ny, nz, nx, toks, width, feats),
        out_shape=(flat, by_head, by_head, by_head),
        in_specs=[pl.BlockSpec(memory_space=pl.ANY)] * 6,
        out_specs=(pl.BlockSpec(memory_space=pltpu.VMEM),) * 4,
        scratch_shapes=scratch,
        compiler_params=pltpu.CompilerParams(collective_id=0, has_side_effects=True),
    )(queries, key_vectors, value_vectors, feature_proj, out_weight, grad_output)
    return pl.pallas_call(
        functools.partial(write_out, heads, width),
        out_shape=(out,) * 4,
        in_specs=[pl.BlockSpec(memory_space=pl.ANY)] * 4,
        compiler_params=pltpu.CompilerParams(vmem_limit_bytes=1 << 20),
        out_specs=(pl.BlockSpec(memory_space=pl.ANY),) * 4,
        scratch_shapes=[pltpu.SemaphoreType.DMA((1 + 3 * heads,))],
    )(*staged)


def solution(mesh):
    rows = P("seq", "head")
    return jax.shard_map(
        local,
        mesh=mesh,
        in_specs=(rows, rows, rows, P("head", None, None), P("head", None), rows),
        out_specs=(rows,) * 4,
        check_vma=False,
    )
```
